512 devices in a mesh: col: 16 (over z_lo, core), row: 32 (over z_hi, x, y).
Axes of the slice: x: 4, y: 4, z: 16 (z_hi: 2, z_lo: 8; z = z_hi * 8 + z_lo), core: 2. Of those that a mesh axis runs over, the one named last changes fastest.
Arguments:
- tokens: bfloat16 [2048, 8192], P('col', 'row'), may hold values from -6 to 6
- gate_weight: bfloat16 [8192, 14336], P('col', 'row'), may hold values from -0.0625 to 0.0625
- up_weight: bfloat16 [8192, 14336], P('col', 'row'), may hold values from -0.0625 to 0.0625
Outputs:
- hidden: bfloat16 [2048, 14336], P('col', 'row')
The draws below stay inside these ranges and needn't reach their ends.
All inputs are finite; a program needn't handle non-finite values.
Results may differ from the reference program's by a relative error of at most 0.0012.
Values may be sent and summed in bfloat16 or wider, within the bound.
No kernel may reach another device: no remote copies, remote signals or barrier semaphores. Data moves between devices by JAX's collectives and lax.ppermute only.
A program may use at most 64 MiB of HBM per device.

```python
import jax
import jax.numpy as jnp

D = 8192
FF = 14336
TOKENS = 2048


def steps_of(key, shape, split, smallest, top_value):
    level = 1.0
    for axis_at, parts in split:
        heights = jax.random.uniform(jax.random.fold_in(jax.random.fold_in(key, 6), axis_at), (parts,), jnp.float32, smallest / len(split), top_value / len(split))
        level = level * jnp.repeat(jnp.exp(heights), shape[axis_at] // parts).reshape((-1,) + (1,) * (len(shape) - 1 - axis_at))
    return level


def normal_values(key, shape, spread, limit, cuts=(), kind=jnp.bfloat16):
    result = spread * jax.random.normal(key, shape, jnp.float32)
    if cuts:
        result = result * steps_of(key, shape, cuts, -0.22, 0.18)
    return jnp.clip(result, -limit, limit).astype(kind)


def setup_inputs(seed: int = 0) -> dict:
    keys = jax.random.split(jax.random.key(seed), 4)
    tokens = normal_values(keys[0], (TOKENS, D), 1.0, 6.0, ((0, 16), (1, 32)))
    gate_weight = normal_values(keys[1], (D, FF), D ** -0.5, 0.0625, ((0, 16), (1, 32)))
    up_weight = normal_values(keys[2], (D, FF), D ** -0.5, 0.0625, ((0, 16), (1, 32)))
    return {"tokens": tokens, "gate_weight": gate_weight, "up_weight": up_weight}


def reference(tokens, gate_weight, up_weight):
    gate = jnp.dot(tokens, gate_weight, preferred_element_type=jnp.float32)
    up = jnp.dot(tokens, up_weight, preferred_element_type=jnp.float32)
    return (jax.nn.silu(gate) * up).astype(jnp.bfloat16)
```

```python
import jax
import jax.numpy as jnp
from jax import lax
from jax.sharding import Mesh, PartitionSpec as P

F32 = jnp.float32
AXES = ("zl", "q", "zh", "x", "y")
SIZES = (8, 2, 2, 4, 4)


def local(tokens, gate_weight, up_weight):
    zl, q = lax.axis_index("zl"), lax.axis_index("q")
    own = (gate_weight.T, up_weight.T)
    other = tuple(lax.ppermute(w, "q", [(0, 1), (1, 0)]) for w in own)

    by_x = lax.all_to_all(tokens.reshape(4, 32, 256), "x", 0, 0, tiled=True)
    by_z = lax.all_to_all(jnp.concatenate([by_x] * 4, 0), ("zh", "zl"), 0, 0, tiled=True)
    mine = lax.dynamic_slice_in_dim(by_z, 8 * (zl // 4), 8, 0)
    whole = lax.all_to_all(jnp.broadcast_to(mine[None], (16, 8, 32, 256)), ("x", "y"), 0, 0, tiled=True)
    rows = whole.reshape(4, 4, 8, 32, 256).transpose(0, 2, 3, 1, 4).reshape(1024, 1024)

    sums = []
    for a, b in zip(own, other):
        w = jnp.where(q == 0, jnp.concatenate([a, b], 1), jnp.concatenate([b, a], 1))
        part = lax.dot_general(rows, w, (((1,), (1,)), ((), ())), preferred_element_type=F32)
        sums.append(part.reshape(4, 8, 32, 448))

    def block(k, at):
        return lax.dynamic_index_in_dim(sums[k], jnp.clip(at, 0, 7), 1, False).reshape(128, 448)

    right = [None, None]
    left = [None, None]
    for s in range(1, 8):
        to_right = [(j, j + 1) for j in range(7) if j <= s - 1]
        to_left = [(j, j - 1) for j in range(1, 8) if j >= 8 - s]
        for k in range(2):
            a, b = block(k, zl + 8 - s), block(k, zl - 8 + s)
            if s > 1:
                r, l = lax.optimization_barrier((right[k], left[k]))
                a, b = a + r, b + l
            right[k] = lax.ppermute(a, "zl", to_right)
            left[k] = lax.ppermute(b, "zl", to_left)
    gate, up = (block(k, zl) + right[k] + left[k] for k in range(2))
    return (jax.nn.silu(gate) * up).astype(jnp.bfloat16)


def solution(mesh):
    fine = Mesh(mesh.devices.reshape(SIZES), AXES)
    spec = P(("zl", "q"), ("zh", "x", "y"))
    return jax.shard_map(local, mesh=fine, in_specs=(spec,) * 3, out_specs=spec, check_vma=False)
```

```python
import jax
import jax.numpy as jnp
from jax import lax
from jax.sharding import Mesh, PartitionSpec as P

F32 = jnp.float32
AXES = ("h", "i", "q", "zh", "x", "y")
SIZES = (2, 4, 2, 2, 4, 4)
SWAP = [(0, 1), (1, 0)]
RING = [(j, (j + 1) % 4) for j in range(4)]


def body(tokens, gate_weight, up_weight):
    h, i, q, zh = (lax.axis_index(a) for a in ("h", "i", "q", "zh"))
    units = [[gate_weight.T], [up_weight.T]]
    for _ in range(3):
        for k in range(2):
            units[k].append(lax.ppermute(units[k][-1], "i", RING))

    far = lax.ppermute(tokens, ("h", "zh"), [(0, 1), (2, 0), (1, 3), (3, 2)])
    near = lax.ppermute(tokens, ("h", "zh"), [(2, 1), (1, 2)])
    near = jnp.where(h == zh, tokens, near)
    two = jnp.where(zh == 0, jnp.stack([near, far]), jnp.stack([far, near]))
    whole = lax.all_to_all(jnp.broadcast_to(two[None], (16, 2, 128, 256)), ("x", "y"), 0, 0, tiled=True)
    whole = whole.reshape(4, 2, 2, 256, 256)
    mine = lax.dynamic_index_in_dim(whole, q, 1, False)
    theirs = lax.ppermute(lax.dynamic_index_in_dim(whole, 1 - q, 1, False), "q", SWAP)
    mine, theirs = (t.transpose(0, 2, 1, 3).reshape(4, 256, 512) for t in (mine, theirs))

    last = (i + 1) & 3

    def dot(t, u, k):
        at = last if u == 3 else (i - u) & 3
        t = lax.dynamic_index_in_dim(t, at, 0, False)
        return lax.dot_general(t, units[k][u], (((1,), (1,)), ((), ())), preferred_element_type=F32)

    both = []
    for k in range(2):
        sent = lax.ppermute(sum(dot(theirs, u, k) for u in range(4)), "q", SWAP)
        total = sum(dot(mine, u, k) for u in range(4)) + sent
        if k:
            total, _ = lax.optimization_barrier((total, away))
        total = total.reshape(2, 128, 448)
        away = (16 * lax.dynamic_index_in_dim(total, 1 - h, 0, False)).astype(jnp.float16)
        keep = lax.dynamic_index_in_dim(total, h, 0, False)
        come = lax.ppermute(away, "h", SWAP)
        both.append(keep + come.astype(F32) / 16)
    gate, up = both
    return (jax.nn.silu(gate) * up).astype(jnp.bfloat16)


def solution(mesh):
    fine = Mesh(mesh.devices.reshape(SIZES), AXES)
    spec = P(("h", "i", "q"), ("zh", "x", "y"))
    return jax.shard_map(body, mesh=fine, in_specs=(spec,) * 3, out_specs=spec, check_vma=False)
```

```python
import jax
import jax.numpy as jnp
from jax import lax
from jax.sharding import Mesh, PartitionSpec as P

F32 = jnp.float32
AXES = ("h", "i", "q", "zh", "x", "y")
SIZES = (2, 4, 2, 2, 4, 4)
SWAP = [(0, 1), (1, 0)]
RING = [(j, (j + 1) % 4) for j in range(4)]


def body(tokens, gate_weight, up_weight):
    h, i, q, zh = (lax.axis_index(a) for a in ("h", "i", "q", "zh"))
    units = [[gate_weight.T], [up_weight.T]]
    for _ in range(3):
        for k in range(2):
            units[k].append(lax.ppermute(units[k][-1], "i", RING))

    edge = lax.ppermute(tokens, ("h", "zh"), [(2, 0), (1, 3)])
    mid = lax.ppermute(tokens, ("h", "zh"), [(2, 1), (1, 2)])
    far = lax.ppermute(tokens, ("h", "zh"), [(0, 1), (3, 2)])
    away = jnp.where(h == zh, edge, mid)
    keep = jnp.where(h == zh, tokens, far)

    def gather(t):
        whole = lax.all_to_all(jnp.broadcast_to(t[None], (16, 128, 256)), ("x", "y"), 0, 0, tiled=True)
        whole = whole.reshape(4, 2, 2, 128, 256)
        theirs = lax.ppermute(lax.dynamic_index_in_dim(whole, 1 - q, 1, False), "q", SWAP)
        mine = lax.dynamic_index_in_dim(whole, q, 1, False)
        wide = [jnp.concatenate([t[:, 0], t[:, 1]], -1) for t in (theirs, mine)]
        return jnp.concatenate(wide, 1)

    away, keep = gather(away), gather(keep)
    last = {}
    for name, n in (("a", 1), ("k", 5)):
        last[name] = (i + n) & 3

    def product(name, t, k):
        total = 0
        for u in range(4):
            at = last[name] if u == 3 else (i - u) & 3
            rows = lax.dynamic_index_in_dim(t, at, 0, False)
            total = total + lax.dot_general(rows, units[k][u], (((1,), (1,)), ((), ())), preferred_element_type=F32)
        return total[128:] + lax.ppermute(total[:128], "q", SWAP)

    come = []
    for k in range(2):
        part = product("a", away, k)
        if k:
            part, _ = lax.optimization_barrier((part, go))
        go = (16 * part).astype(jnp.float16)
        come.append(lax.ppermute(go, "h", SWAP))
    gate, up = (product("k", keep, k) + come[k].astype(F32) / 16 for k in range(2))
    return (jax.nn.silu(gate) * up).astype(jnp.bfloat16)


def solution(mesh):
    fine = Mesh(mesh.devices.reshape(SIZES), AXES)
    spec = P(("h", "i", "q"), ("zh", "x", "y"))
    return jax.shard_map(body, mesh=fine, in_specs=(spec,) * 3, out_specs=spec, check_vma=False)
```
